256 devices in a mesh: slab: 16 (over z_hi, x, core), chan: 16 (over y, z_lo).
Axes of the slice: x: 4, y: 4, z: 8 (z_hi: 2, z_lo: 4; z = z_hi * 4 + z_lo), core: 2. Of those that a mesh axis runs over, the one named last changes fastest.
Arguments:
- activations: bfloat16 [2, 128, 32, 16384], P(None, 'chan', 'slab'), may hold values from -6 to 6
- out_grad: bfloat16 [2, 256, 16, 4096], P(None, 'chan', 'slab'), may hold values from -6 to 6
- weights: bfloat16 [27, 128, 256], P(None, 'chan'), may hold values from -0.109375 to 0.109375
Outputs:
- input_grad: bfloat16 [2, 128, 32, 16384], P(None, 'chan', 'slab')
- weight_grad: float32 [27, 128, 256], P(None, 'chan', 'slab')
The draws below stay inside these ranges and needn't reach their ends.
All inputs are finite; a program needn't handle non-finite values.
Results may differ from the reference program's by a relative error of at most 0.001.
Values may be sent and summed in bfloat16 or wider, within the bound.
A program may use at most 128 MiB of HBM per device.

```python
import math
import jax
import jax.numpy as jnp
from jax import lax

CIN = 128
COUT = 256
EDGE = 128
SAMPLES = 2
DEPTH = 32


def strengthened(result, stream_key, source, target, shards_of, factor):
    def block_of(position):
        return (jnp.arange(result.shape[position]) // (result.shape[position] // shards_of)).reshape((-1,) + (1,) * (result.ndim - 1 - position))

    one_side = jax.random.permutation(stream_key, shards_of)[block_of(target)]
    second = (block_of(target) + shards_of // 2) % shards_of
    return jnp.where((block_of(source) == one_side) | (block_of(source) == second), factor * result, result)


def block_scale(own_key, shape, cuts, least, high):
    def one(axis_at, blocks):
        draws = jax.random.uniform(jax.random.fold_in(jax.random.fold_in(own_key, 6), axis_at), (blocks,), jnp.float32, least / len(cuts), high / len(cuts))
        return jnp.repeat(jnp.exp(draws), shape[axis_at] // blocks).reshape((-1,) + (1,) * (len(shape) - axis_at - 1))

    factor_of = one(*cuts[0])
    for cut in cuts[1:]:
        factor_of = factor_of * one(*cut)
    return factor_of


def centred(key, shape, spread, bound, split=(), kind=jnp.bfloat16):
    array = spread * jax.random.normal(key, shape, jnp.float32)
    if split:
        array = array * block_scale(key, shape, split, -0.22, 0.18)
    return jnp.clip(array, -bound, bound).astype(kind)


def heavy_noise(stream_key, dims, scale, most, cuts, heavy, held_as=jnp.bfloat16):
    array = scale * jax.random.normal(stream_key, dims, jnp.float32)
    if cuts:
        array = array * block_scale(stream_key, dims, cuts, -0.22, 0.18)
    return jnp.clip(strengthened(array, jax.random.fold_in(stream_key, 3), *heavy), -most, most).astype(held_as)


def setup_inputs(seed: int = 0) -> dict:
    seeds = jax.random.split(jax.random.key(seed), 4)
    return {
        "activations": centred(seeds[0], (SAMPLES, CIN, DEPTH, EDGE * EDGE), 1.0, 6.0, ((1, 16), (2, 16))),
        "out_grad": heavy_noise(seeds[1], (SAMPLES, COUT, DEPTH // 2, (EDGE // 2) * (EDGE // 2)), 1.0, 6.0, ((1, 16), (2, 16)), (2, 1, 16, 2.0)),
        "weights": centred(seeds[2], (27, CIN, COUT), (27 * CIN) ** -0.5, 0.109375, ((1, 16),)),
    }


def shift_back(values, which_axis):
    extent = list(values.shape)
    extent[which_axis] = 1
    zero_slab = jnp.zeros(tuple(extent), values.dtype)
    retained = lax.slice_in_dim(values, 0, values.shape[which_axis] - 1, axis=which_axis)
    return jnp.concatenate([zero_slab, retained], axis=which_axis)

def shift_ahead(values, which_axis):
    extent = list(values.shape)
    extent[which_axis] = 1
    zero_slab = jnp.zeros(tuple(extent), values.dtype)
    retained = lax.slice_in_dim(values, 1, values.shape[which_axis], axis=which_axis)
    return jnp.concatenate([retained, zero_slab], axis=which_axis)

def flat_back(values, amount):
    zero_part = jnp.zeros(values.shape[:-1] + (amount,), values.dtype)
    return jnp.concatenate([zero_part, values[..., :values.shape[-1] - amount]], axis=-1)

def flat_ahead(values, amount):
    zero_part = jnp.zeros(values.shape[:-1] + (amount,), values.dtype)
    return jnp.concatenate([values[..., amount:], zero_part], axis=-1)

def column_index(length, half_edge):
    return lax.iota(jnp.int32, length) % half_edge

def tap_view(volume, row_tap, col_tap, half_edge):
    cells = half_edge * half_edge
    row_phase = 0 if row_tap == 1 else 1
    col_phase = 0 if col_tap == 1 else 1
    block = row_phase * 2 + col_phase
    picked = volume[..., block * cells:(block + 1) * cells]
    if row_tap == 0:
        picked = flat_back(picked, half_edge)
    if col_tap == 0:
        picked = flat_back(picked, 1)
        keep_mask = column_index(cells, half_edge) != 0
        picked = jnp.where(keep_mask, picked, jnp.zeros_like(picked))
    return picked

def assemble(fetch, half_edge, block_cells, keep):
    last_column = column_index(block_cells, half_edge) == half_edge - 1

    def col_ahead(values):
        moved = flat_ahead(values, 1)
        return jnp.where(last_column, jnp.zeros_like(moved), moved)
    rows_even = [fetch(1, col_tap) for col_tap in range(3)]
    rows_odd = [fetch(2, col_tap) + flat_ahead(fetch(0, col_tap), half_edge) for col_tap in range(3)]
    phases = []
    for rows in (rows_even, rows_odd):
        phases.append(rows[1][..., :keep])
        phases.append((rows[2] + col_ahead(rows[0]))[..., :keep])
    return jnp.concatenate(phases, axis=-1)

def reference(activations, out_grad, weights):
    half_edge = EDGE // 2
    cells = half_edge * half_edge
    phased = activations.astype(jnp.float32).reshape(SAMPLES, CIN, DEPTH // 2, 2, EDGE * EDGE)
    even_planes = phased[:, :, :, 0]
    odd_planes = phased[:, :, :, 1]
    depth_views = (shift_back(odd_planes, 2), even_planes, odd_planes)
    signal = out_grad.astype(jnp.float32)
    signal_next = shift_ahead(signal, 2)
    grad_scale = 1.0 / math.sqrt(SAMPLES * (DEPTH // 2) * half_edge * half_edge)
    pieces = []
    for depth_tap in range(3):
        for row_tap in range(3):
            for col_tap in range(3):
                view = tap_view(depth_views[depth_tap], row_tap, col_tap, half_edge)
                pieces.append(jnp.einsum('bcdp,bkdp->ck', view, signal))
    weight_grad = jnp.stack(pieces) * grad_scale
    weights_wide = weights.astype(jnp.float32)
    folded = []
    for depth_tap in range(3):
        source = signal_next if depth_tap == 0 else signal

        def fetch(row_tap, col_tap, depth_tap=depth_tap, source=source):
            return jnp.einsum('ck,bkdp->bcdp', weights_wide[9 * depth_tap + 3 * row_tap + col_tap], source)
        folded.append(assemble(fetch, half_edge, cells, cells))
    odd_out = folded[2] + folded[0]
    input_grad = jnp.stack([folded[1], odd_out], axis=3).reshape(SAMPLES, CIN, DEPTH, EDGE * EDGE).astype(jnp.bfloat16)
    return (input_grad, weight_grad)
```

```python
import functools
import math

import jax
import jax.numpy as jnp
from jax import lax
from jax.experimental import pallas as pl
from jax.experimental.pallas import tpu as pltpu
from jax.sharding import PartitionSpec as P

EDGE = 128
MESH = pl.DeviceIdType.MESH
ROW = 4


def remote(src, dst, send_sem, recv_sem, axis, target):
    return pltpu.make_async_remote_copy(
        src_ref=src,
        dst_ref=dst,
        send_sem=send_sem,
        recv_sem=recv_sem,
        device_id={axis: target},
        device_id_type=MESH,
    )


def gather_kernel(own_ref, out_ref, local_sem, zs, zr, ys, yr, fs, fr):
    me = lax.axis_index("chan")
    y, z = me // ROW, me % ROW
    rows = own_ref.shape[1]

    def device(y_at, z_at):
        return ROW * (y_at % ROW) + z_at % ROW

    def slot(index):
        return pl.ds(pl.multiple_of(index * rows, rows), rows)

    ahead, behind = device(y + 1, z), device(y + ROW - 1, z)
    z_peers = [device(y, z + k) for k in range(1, ROW)]
    barrier = pltpu.get_barrier_semaphore()
    for peer in [ahead, behind] + z_peers:
        pl.semaphore_signal(barrier, inc=1, device_id={"chan": peer}, device_id_type=MESH)
    pl.semaphore_wait(barrier, 5)

    sent = []

    def start(copy):
        copy.start()
        sent.append(copy)
        return copy

    mine = out_ref.at[:, slot(me), :]
    local = pltpu.make_async_copy(own_ref, mine, local_sem)

    def y_send(j):
        block = device(y, z + ROW - j)
        place = out_ref.at[:, slot(block), :]
        source = own_ref if j == 0 else place
        return [
            start(remote(source, place, ys.at[2 * j + d], yr.at[2 * j + d], "chan", peer))
            for d, peer in enumerate((ahead, behind))
        ]

    def forward(j, copies):
        result = []
        for d, peer in enumerate((ahead, behind)):
            copies[d].wait_recv()
            block = device(y + (ROW - 1, 1)[d], z + ROW - j)
            place = out_ref.at[d, slot(block), :]
            result.append(start(remote(place, place, fs.at[2 * j + d], fr.at[2 * j + d], "chan", peer)))
        return result

    direct = {0: y_send(0)}
    along = {}
    for k in (1, 3, 2):
        along[k] = start(remote(own_ref, mine, zs.at[k - 1], zr.at[k - 1], "chan", z_peers[k - 1]))
    local.start()
    forwarded = forward(0, direct[0])
    along[1].wait_recv()
    direct[1] = y_send(1)
    along[3].wait_recv()
    direct[3] = y_send(3)
    forwarded += forward(1, direct[1])
    along[2].wait_recv()
    direct[2] = y_send(2)
    forwarded += forward(3, direct[3])
    forwarded += forward(2, direct[2])
    for copy in forwarded:
        copy.wait_recv()
    for copy in sent:
        copy.wait_send()
    local.wait()


def gather(own):
    samples, rows, cells = own.shape
    count = ROW * ROW
    dma = pltpu.SemaphoreType.DMA
    return pl.pallas_call(
        gather_kernel,
        out_shape=jax.ShapeDtypeStruct((samples, rows * count, cells), own.dtype),
        in_specs=[pl.BlockSpec(memory_space=pltpu.VMEM)],
        out_specs=pl.BlockSpec(memory_space=pl.ANY),
        scratch_shapes=[dma, dma((3,)), dma((3,)), dma((8,)), dma((8,)), dma((8,)), dma((8,))],
        compiler_params=pltpu.CompilerParams(collective_id=0, has_side_effects=True),
    )(own)


def scatter_sum_kernel(scale, parts_ref, out_ref, held, send_sem, recv_sem):
    count = parts_ref.shape[0]
    me = lax.axis_index("slab")
    barrier = pltpu.get_barrier_semaphore()
    for k in range(1, count):
        peer = (me + k) % count
        pl.semaphore_signal(barrier, inc=1, device_id={"slab": peer}, device_id_type=MESH)
    pl.semaphore_wait(barrier, count - 1)
    copies = []
    for k in range(1, count):
        peer = (me + k) % count
        copy = remote(parts_ref.at[peer], held.at[k - 1], send_sem.at[k - 1], recv_sem.at[k - 1], "slab", peer)
        copy.start()
        copies.append(copy)
    total = parts_ref[me]
    for k in range(1, count):
        copies[k - 1].wait_recv()
        total += held[k - 1]
    out_ref[...] = total * scale
    for copy in copies:
        copy.wait_send()


def scatter_sum(parts, scale):
    count, rows, lanes = parts.shape
    dma = pltpu.SemaphoreType.DMA
    return pl.pallas_call(
        functools.partial(scatter_sum_kernel, scale),
        out_shape=jax.ShapeDtypeStruct((rows, lanes), parts.dtype),
        in_specs=[pl.BlockSpec(memory_space=pltpu.VMEM)],
        out_specs=pl.BlockSpec(memory_space=pltpu.VMEM),
        scratch_shapes=[
            pltpu.VMEM((count - 1, rows, lanes), parts.dtype),
            dma((count - 1,)),
            dma((count - 1,)),
        ],
        compiler_params=pltpu.CompilerParams(collective_id=1, has_side_effects=True),
    )(parts)


def from_behind(x, axis, by):
    count = lax.axis_size(axis)
    pairs = [(i, i + by) for i in range(count) if 0 <= i + by < count]
    return lax.ppermute(x, axis, pairs)


def flat_back(values, amount):
    zero_part = jnp.zeros(values.shape[:-1] + (amount,), values.dtype)
    return jnp.concatenate([zero_part, values[..., : values.shape[-1] - amount]], axis=-1)


def flat_ahead(values, amount):
    zero_part = jnp.zeros(values.shape[:-1] + (amount,), values.dtype)
    return jnp.concatenate([values[..., amount:], zero_part], axis=-1)


def column_index(length, half_edge):
    return lax.iota(jnp.int32, length) % half_edge


def tap_view(volume, row_tap, col_tap, half_edge):
    cells = half_edge * half_edge
    row_phase = 0 if row_tap == 1 else 1
    col_phase = 0 if col_tap == 1 else 1
    block = row_phase * 2 + col_phase
    picked = volume[..., block * cells : (block + 1) * cells]
    if row_tap == 0:
        picked = flat_back(picked, half_edge)
    if col_tap == 0:
        picked = flat_back(picked, 1)
        keep_mask = column_index(cells, half_edge) != 0
        picked = jnp.where(keep_mask, picked, jnp.zeros_like(picked))
    return picked


def assemble(fetch, half_edge, block_cells):
    last_column = column_index(block_cells, half_edge) == half_edge - 1
    rows_even = [fetch(1, col_tap) for col_tap in range(3)]
    rows_odd = [
        fetch(2, col_tap) + flat_ahead(fetch(0, col_tap), half_edge) for col_tap in range(3)
    ]
    phases = []
    for rows in (rows_even, rows_odd):
        phases.append(rows[1])
        moved = flat_ahead(rows[0], 1)
        phases.append(rows[2] + jnp.where(last_column, jnp.zeros_like(moved), moved))
    return jnp.concatenate(phases, axis=-1)


def body(activations, out_grad, weights):
    samples, chan_local, planes, plane_cells = activations.shape
    half_edge = EDGE // 2
    cells = half_edge * half_edge
    out_planes = planes // 2
    phased = activations.reshape(samples, chan_local, out_planes, 2, plane_cells)
    even_planes = phased[:, :, :, 0]
    odd_planes = phased[:, :, :, 1]
    previous = from_behind(odd_planes[:, :, out_planes - 1], "slab", 1)
    odd_before = jnp.concatenate([previous[:, :, None], odd_planes[:, :, : out_planes - 1]], axis=2)
    depth_views = (odd_before, even_planes, odd_planes)
    own_planes = gather(out_grad[:, :, 0])[:, :, None]
    pieces = []
    for depth_tap in range(3):
        stacked = jnp.stack(
            [
                tap_view(depth_views[depth_tap], row_tap, col_tap, half_edge)
                for row_tap in range(3)
                for col_tap in range(3)
            ]
        )
        pieces.append(
            jnp.einsum("tbcdp,bkdp->tck", stacked, own_planes, preferred_element_type=jnp.float32)
        )
    local_grad = jnp.concatenate(pieces, axis=0)
    count = lax.axis_size("slab")
    total_cells = samples * out_planes * count * half_edge * half_edge
    taps, chan_rows, columns = local_grad.shape
    parts = local_grad.reshape(taps, chan_rows, count, columns // count).transpose(2, 0, 1, 3)
    parts = parts.reshape(count, taps, chan_rows * columns // count)
    weight_grad = scatter_sum(parts, 1.0 / math.sqrt(total_cells)).reshape(taps, chan_rows, columns // count)
    folded = []
    for depth_tap in range(3):
        groups = jnp.einsum(
            "tck,bkdp->tbcdp",
            weights[9 * depth_tap : 9 * depth_tap + 9],
            own_planes,
            preferred_element_type=jnp.float32,
        )

        def fetch(row_tap, col_tap, groups=groups):
            return groups[3 * row_tap + col_tap]

        folded.append(assemble(fetch, half_edge, cells))
    shifted = from_behind(folded[0], "slab", -1)
    odd_out = folded[2] + shifted
    chan_rows = folded[1].shape[1]
    kept_cells = 4 * cells
    local_grad_in = (
        jnp.stack([folded[1], odd_out], axis=3)
        .reshape(samples, chan_rows, planes, kept_cells)
        .astype(jnp.bfloat16)
    )
    return (local_grad_in, weight_grad)


def solution(mesh):
    placed = (P(None, "chan", "slab", None), P(None, "chan", "slab", None), P(None, "chan", None))
    return jax.shard_map(
        body,
        mesh=mesh,
        in_specs=placed,
        out_specs=(P(None, "chan", "slab", None), P(None, "chan", "slab")),
        check_vma=False,
    )
```
